32 devices in a mesh: groups: 2 (over x), replica: 8 (over z, y), channel: 2 (over core).
Axes of the slice: x: 2, y: 2, z: 4, core: 2. Of those that a mesh axis runs over, the one named last changes fastest.
Arguments:
- queries: bfloat16 [16, 2, 32, 4096], P(('groups', 'replica'), None, None, 'channel'), parts along dimension 0, may hold values from -360 to 360
- new_kv: bfloat16 [16, 2, 32, 1024], P(('groups', 'replica'), None, None, 'channel'), parts along dimension 0, may hold values from -6 to 6
- cached_lookup_pairs: bfloat16 [16, 1024, 1024], P(('groups', 'replica'), None, 'channel'), parts along dimension 0, may hold values from -6 to 6
- prefix_ssm: bfloat16 [16, 16, 8192], P(('groups', 'replica'), None, 'channel'), parts along dimension 0, may hold values from -6 to 6
- prefix_conv: bfloat16 [16, 3, 8192], P(('groups', 'replica'), None, 'channel'), parts along dimension 0, may hold values from -6 to 6
- pool_kv: bfloat16 [16, 4, 256, 1024], P(('groups', 'replica'), None, None, 'channel'), parts along dimension 0, may hold values from -6 to 6
- pool_ssm: bfloat16 [16, 16, 8192], P(('groups', 'replica'), None, 'channel'), parts along dimension 0, may hold values from -6 to 6
- pool_conv: bfloat16 [16, 3, 8192], P(('groups', 'replica'), None, 'channel'), parts along dimension 0, may hold values from -6 to 6
- owner_id: int32 [2], P('groups'), parts along dimension 0, may hold values from 0 to 7
- readers: int32 [16], P(('groups', 'replica')), parts along dimension 0, may hold values 0 or 1
- restore_src: int32 [16, 4], P('groups'), parts along dimension 0, may hold values from 0 to 7, as said below
- restore_blk: int32 [16, 4], P('groups'), parts along dimension 0, may hold values from 0 to 3, as said below
- state_src: int32 [16], P('groups'), parts along dimension 0, may hold values from 0 to 7, as said below
- ctx_blocks: int32 [16], P(('groups', 'replica')), parts along dimension 0, may hold values from 1 to 4, as said below
- mamba_x: bfloat16 [16, 2, 32, 8192], P(('groups', 'replica'), None, None, 'channel'), parts along dimension 0, may hold values from -6 to 6
- mamba_z: bfloat16 [16, 2, 32, 8192], P(('groups', 'replica'), None, None, 'channel'), parts along dimension 0, may hold values from -6 to 6
- mamba_dt: bfloat16 [16, 2, 32, 8192], P(('groups', 'replica'), None, None, 'channel'), parts along dimension 0, may hold values from -2 to 8
- dt_bias: float32 [8192], P('channel'), may hold values from -6 to -2.5
- a_log: float32 [16, 8192], P(None, 'channel'), may hold values from 0 to 2
- bypass_gain: float32 [8192], P('channel'), may hold values from 0.5 to 1.5
- conv_w: float32 [4, 8192], P(None, 'channel'), may hold values from -3 to 3
- conv_b: float32 [8192], P('channel'), may hold values from -0.5 to 0.5
- w_bc: bfloat16 [8192, 32], P('channel'), may hold values from -0.0625 to 0.0625
Outputs:
- attention_out: bfloat16 [16, 2, 32, 4096], P(('groups', 'replica'), None, None, 'channel'), parts along dimension 0
- mamba_out: bfloat16 [16, 2, 32, 8192], P(('groups', 'replica'), None, None, 'channel'), parts along dimension 0
The draws below stay inside these ranges and needn't reach their ends.
There are 2 independent parts, one for each index of `groups`. The reference program is written for one: setup_inputs(seed, part) draws one part's arguments, and reference() takes and returns one part's arrays. A program takes and returns all parts, laid end to end along the dimension named above; an argument that names none is the same for every part. Nothing has to cross between parts.
Inputs may be any that keep to these rules, and one draw needn't show every extreme that they name: `restore_src`: each row names 4 different replicas, and each replica is named in exactly 4 rows, so at most one block goes from one replica to one row's replica. Every pair (restore_src, restore_blk) is different: each stored block of each replica is listed exactly once. `state_src`: A permutation of the replicas. Only slots j < ctx_blocks[d] of row d are read; some replica has 4.
All inputs are finite; a program needn't handle non-finite values. No bound on the sum of `readers` on one device may be relied on, other than what follows from the above.
Results may differ from the reference program's by a relative error of at most 0.0049.
Values may be sent and summed in bfloat16 or wider, within the bound.
A program may use at most 128 MiB of HBM per device.

```python
import jax
import jax.numpy as jnp
from jax import lax

HD = 128
KV_HEADS = 4
Q_PER_KV = 8
Q_HEADS = 32
KVW = 1024
INNER = 8192
STATE = 16
CONV = 4
BLOCK = 256
MAXB = 4
POOL = 4
PREFIX = 1024
NEW = 32
N_REPLICA = 8


def restore_tables(key):
    base = jax.random.fold_in(key, 7031)
    key_a, key_b, key_c, key_d = jax.random.split(base, 4)
    labels = jax.random.permutation(key_a, N_REPLICA)
    slots = jax.random.permutation(key_b, N_REPLICA)
    offsets = jax.random.permutation(key_c, N_REPLICA)[:MAXB]
    sources = labels[(slots[:, None] + offsets[None, :]) % N_REPLICA]
    orders = jax.vmap(lambda sub_key: jax.random.permutation(sub_key, MAXB))(jax.random.split(key_d, N_REPLICA))
    blocks = orders[sources, jnp.arange(MAXB)[None, :]]
    return (sources.astype(jnp.int32), blocks.astype(jnp.int32))


def draw_restore_src(key, part):
    return restore_tables(key)[0]


def draw_restore_blk(key, part):
    return restore_tables(key)[1]


def draw_state_src(key, part):
    return jax.random.permutation(jax.random.fold_in(key, 9127), N_REPLICA).astype(jnp.int32)


def draw_ctx_blocks(key, part):
    base = jax.random.fold_in(key, 4409)
    key_a, key_b = jax.random.split(base)
    payload_lines = jax.random.randint(key_a, (N_REPLICA,), MAXB - 3, MAXB + 1)
    chosen = jax.random.randint(key_b, (), 0, N_REPLICA)
    return jnp.where(jnp.arange(N_REPLICA) == chosen, MAXB, payload_lines).astype(jnp.int32)


def draw_queries(key, part):
    base = jax.random.fold_in(key, 2203)
    key_a = jax.random.fold_in(base, 0)
    payload_lines = jnp.clip(jax.random.normal(key_a, (N_REPLICA, 2, NEW, Q_HEADS * HD), jnp.float32), -6.0, 6.0)
    return payload_lines.astype(jnp.bfloat16)


def draw_mamba_dt(key, part):
    base = jax.random.fold_in(key, 5581)
    key_a, key_b = jax.random.split(base)
    shape = (N_REPLICA, 2, NEW, INNER)
    payload_lines = jnp.clip(0.5 * jax.random.normal(key_a, shape, jnp.float32), -2.0, 2.0)
    destination_places = jax.random.randint(key_b, (N_REPLICA, 2, 3), 0, NEW)
    update_order = jnp.arange(NEW)[None, None, None, :]
    copy_batches = jnp.sum((destination_places[..., None] == update_order).astype(jnp.float32), axis=2)
    return (payload_lines + 2.0 * copy_batches[..., None]).astype(jnp.bfloat16)


def plant(entries, rng, low, largest):
    longest = entries.shape.index(max(entries.shape))
    spots = []
    for shift in (0, 1):
        where = [jax.random.randint(jax.random.fold_in(rng, axis), (), 0, length) for axis, length in enumerate(entries.shape)]
        where[longest] = (where[longest] + shift) % entries.shape[longest]
        spots.append(tuple(where))
    return entries.at[spots[0]].set(low).at[spots[1]].set(largest)


def block_levels(own_key, shape, cuts, low, largest):
    loudness, own = 1.0, jax.random.fold_in(own_key, 6)
    for position, blocks in cuts:
        steps = jnp.exp(jax.random.uniform(jax.random.fold_in(own, position), (blocks,), jnp.float32, low / len(cuts), largest / len(cuts)))
        loudness = loudness * jnp.repeat(steps, shape[position] // blocks).reshape([-1 if axis == position else 1 for axis in range(len(shape))])
    return loudness


def noise(key, extent, deviation, limit, shards=(), kind=jnp.bfloat16):
    factor_of = block_levels(key, extent, shards, -0.22, 0.18) if shards else 1.0
    values = jax.random.normal(key, extent, jnp.float32) * deviation * factor_of
    return jnp.minimum(jnp.maximum(values, -limit), limit).astype(kind)


def setup_inputs(seed: int = 0, part: int = 0) -> dict:
    seeds = jax.random.split(jax.random.key(seed), 24)
    part_keys = jax.random.split(jax.random.fold_in(seeds[23], part), 24)
    queries = draw_queries(jax.random.fold_in(jax.random.fold_in(seeds[23], part), 71), part)
    new_kv = noise(part_keys[1], (N_REPLICA, 2, NEW, KVW), 1.0, 6.0, ((0, 8), (3, 2)))
    cached_lookup_pairs = noise(part_keys[2], (N_REPLICA, PREFIX, KVW), 1.0, 6.0, ((0, 8), (2, 2)))
    prefix_ssm = noise(part_keys[3], (N_REPLICA, STATE, INNER), 1.0, 6.0, ((0, 8), (2, 2)))
    prefix_conv = noise(part_keys[4], (N_REPLICA, CONV - 1, INNER), 1.0, 6.0, ((0, 8), (2, 2)))
    pool_kv = noise(part_keys[5], (N_REPLICA, POOL, BLOCK, KVW), 1.0, 6.0, ((0, 8), (3, 2)))
    pool_ssm = noise(part_keys[6], (N_REPLICA, STATE, INNER), 1.0, 6.0, ((0, 8), (2, 2)))
    pool_conv = noise(part_keys[7], (N_REPLICA, CONV - 1, INNER), 1.0, 6.0, ((0, 8), (2, 2)))
    owner_id = jax.random.randint(part_keys[8], (1,), 0, N_REPLICA).astype(jnp.int32)
    readers = plant((jax.random.randint(part_keys[9], (N_REPLICA,), 0, 4) < 3).astype(jnp.int32), jax.random.fold_in(part_keys[9], 1), 0, 1)
    restore_src = draw_restore_src(jax.random.fold_in(jax.random.fold_in(seeds[23], part), 71), part)
    restore_blk = draw_restore_blk(jax.random.fold_in(jax.random.fold_in(seeds[23], part), 71), part)
    state_src = draw_state_src(jax.random.fold_in(jax.random.fold_in(seeds[23], part), 71), part)
    ctx_blocks = draw_ctx_blocks(jax.random.fold_in(jax.random.fold_in(seeds[23], part), 71), part)
    mamba_x = noise(part_keys[14], (N_REPLICA, 2, NEW, INNER), 1.0, 6.0, ((0, 8), (3, 2)))
    mamba_z = noise(part_keys[15], (N_REPLICA, 2, NEW, INNER), 1.0, 6.0, ((0, 8), (3, 2)))
    mamba_dt = draw_mamba_dt(jax.random.fold_in(jax.random.fold_in(seeds[23], part), 71), part)
    dt_bias = jnp.clip(-6.0 + 3.5 * jax.random.uniform(seeds[17], (INNER,), jnp.float32) ** block_levels(seeds[17], (INNER,), ((0, 2),), -0.2, 0.2), -6.0, -2.5)
    a_log = jnp.clip(2.0 * jax.random.uniform(seeds[18], (STATE, INNER), jnp.float32) ** block_levels(seeds[18], (STATE, INNER), ((1, 2),), -0.2, 0.2), 0.0, 2.0)
    bypass_gain = jnp.clip(0.5 + 1.0 * jax.random.uniform(seeds[19], (INNER,), jnp.float32) ** block_levels(seeds[19], (INNER,), ((0, 2),), -0.2, 0.2), 0.5, 1.5)
    conv_w = noise(seeds[20], (CONV, INNER), CONV ** -0.5, 3.0, ((1, 2),), jnp.float32)
    conv_b = jnp.clip(jax.random.uniform(seeds[21], (INNER,), jnp.float32, -0.5, 0.5) * block_levels(seeds[21], (INNER,), ((0, 2),), -0.4, 0.0), -0.5, 0.5)
    w_bc = noise(seeds[22], (INNER, 2 * STATE), INNER ** -0.5, 0.0625, ((0, 2),))
    return {"queries": queries, "new_kv": new_kv, "cached_lookup_pairs": cached_lookup_pairs, "prefix_ssm": prefix_ssm, "prefix_conv": prefix_conv, "pool_kv": pool_kv, "pool_ssm": pool_ssm, "pool_conv": pool_conv, "owner_id": owner_id, "readers": readers, "restore_src": restore_src, "restore_blk": restore_blk, "state_src": state_src, "ctx_blocks": ctx_blocks, "mamba_x": mamba_x, "mamba_z": mamba_z, "mamba_dt": mamba_dt, "dt_bias": dt_bias, "a_log": a_log, "bypass_gain": bypass_gain, "conv_w": conv_w, "conv_b": conv_b, "w_bc": w_bc}


def attend(query_rows, context, live_keys, fresh_keys):
    factor = query_rows.shape[-1] ** -0.5
    rows_f = query_rows.astype(jnp.float32)
    scores_ctx = jnp.einsum("qhgd,khd->hgqk", rows_f, context[:, :, 0].astype(jnp.float32)) * factor
    scores_ctx = jnp.where(live_keys, scores_ctx, -jnp.inf)
    scores_new = jnp.einsum("qhgd,khd->hgqk", rows_f, fresh_keys[:, :, 0].astype(jnp.float32)) * factor
    new_count = fresh_keys.shape[0]
    causal = lax.broadcasted_iota(jnp.int32, (new_count, new_count), 0) >= lax.broadcasted_iota(jnp.int32, (new_count, new_count), 1)
    scores_new = jnp.where(causal, scores_new, -jnp.inf)
    highest = jnp.maximum(jnp.max(scores_ctx, axis=-1, keepdims=True), jnp.max(scores_new, axis=-1, keepdims=True))
    weight_ctx = jnp.exp(scores_ctx - highest)
    weight_new = jnp.exp(scores_new - highest)
    denominator = jnp.sum(weight_ctx, axis=-1) + jnp.sum(weight_new, axis=-1)
    scaled_product = jnp.einsum("hgqk,khd->qhgd", weight_ctx.astype(jnp.bfloat16).astype(jnp.float32), context[:, :, 1].astype(jnp.float32))
    scaled_product = scaled_product + jnp.einsum("hgqk,khd->qhgd", weight_new.astype(jnp.bfloat16).astype(jnp.float32), fresh_keys[:, :, 1].astype(jnp.float32))
    result = scaled_product / jnp.transpose(denominator, (2, 0, 1))[..., None]
    return result.astype(jnp.bfloat16).reshape(new_count, -1)


def reference(queries, new_kv, cached_lookup_pairs, prefix_ssm, prefix_conv, pool_kv, pool_ssm, pool_conv, owner_id, readers, restore_src, restore_blk, state_src, ctx_blocks, mamba_x, mamba_z, mamba_dt, dt_bias, a_log, bypass_gain, conv_w, conv_b, w_bc):
    owner_pos = owner_id[0]
    shared_kv = cached_lookup_pairs[owner_pos]
    shared_ssm = prefix_ssm[owner_pos].astype(jnp.float32)
    shared_conv = prefix_conv[owner_pos].astype(jnp.float32)
    decay_rate = -jnp.exp(a_log)
    w_bc_f = w_bc.astype(jnp.float32)

    def serve_one(replica_pos):
        reading_replica = readers[replica_pos] > 0
        grouped = queries[replica_pos].reshape(2, NEW, KV_HEADS, Q_PER_KV, HD)
        fresh_kv = new_kv[replica_pos].reshape(2, NEW, KV_HEADS, 2, HD)
        prefix_ctx = shared_kv.reshape(PREFIX, KV_HEADS, 2, HD)
        fresh_out = attend(grouped[0], prefix_ctx, jnp.broadcast_to(reading_replica, (PREFIX,)), fresh_kv[0])
        sources = restore_src[replica_pos]
        blocks = restore_blk[replica_pos]
        restored = pool_kv[sources, blocks].reshape(MAXB * BLOCK, KV_HEADS, 2, HD)
        live_keys = jnp.arange(MAXB * BLOCK, dtype=jnp.int32) < ctx_blocks[replica_pos] * BLOCK
        resumed_out = attend(grouped[1], restored, live_keys, fresh_kv[1])
        holder = state_src[replica_pos]
        start_ssm = jnp.stack([jnp.where(reading_replica, shared_ssm, 0.0), pool_ssm[holder].astype(jnp.float32)])
        start_conv = jnp.stack([jnp.where(reading_replica, shared_conv, 0.0), pool_conv[holder].astype(jnp.float32)])
        padded = jnp.concatenate([start_conv, mamba_x[replica_pos].astype(jnp.float32)], axis=1)
        conv_sum = conv_b + conv_w[0] * padded[:, 0:NEW]
        for offset in range(1, CONV):
            conv_sum = conv_sum + conv_w[offset] * padded[:, offset:offset + NEW]
        signal = jax.nn.silu(conv_sum)
        signal_round = lax.optimization_barrier(signal.astype(jnp.bfloat16)).astype(jnp.float32)
        state_bc = jnp.einsum("rtc,cs->rts", signal_round, w_bc_f)
        input_gain = state_bc[..., :STATE]
        readout = state_bc[..., STATE:]
        step_size = jax.nn.softplus(mamba_dt[replica_pos].astype(jnp.float32) + dt_bias)

        def advance(hidden, inputs):
            step_now, signal_now, gain_now, readout_now = inputs
            hidden = jnp.exp(step_now[:, None, :] * decay_rate) * hidden + gain_now[:, :, None] * (step_now * signal_now)[:, None, :]
            result = jnp.sum(readout_now[:, :, None] * hidden, axis=1) + bypass_gain * signal_now
            return hidden, result

        ignored, outputs = lax.scan(advance, start_ssm, (jnp.swapaxes(step_size, 0, 1), jnp.swapaxes(signal, 0, 1), jnp.swapaxes(input_gain, 0, 1), jnp.swapaxes(readout, 0, 1)))
        gated = (jnp.swapaxes(outputs, 0, 1) * jax.nn.silu(mamba_z[replica_pos].astype(jnp.float32))).astype(jnp.bfloat16)
        return jnp.stack([fresh_out, resumed_out]), gated

    attention_out, mamba_out = lax.map(serve_one, jnp.arange(N_REPLICA, dtype=jnp.int32))
    return attention_out, mamba_out
```

```python
import jax
import jax.numpy as jnp
from jax import lax
from jax.experimental import pallas as pl
from jax.experimental.pallas import tpu as pltpu
from jax.sharding import PartitionSpec as P

HD = 128
Q_PER_KV = 8
KV_CHUNKS = 8
MESH = pl.DeviceIdType.MESH


def scores_of(keys, query):
    contract = (((1,), (1,)), ((), ()))
    return lax.dot_general(keys, query, contract, preferred_element_type=jnp.float32) * (HD ** (-0.5))


def mix(values, weight):
    contract = (((0,), (0,)), ((), ()))
    return lax.dot_general(values, weight.astype(jnp.bfloat16), contract, preferred_element_type=jnp.float32)


def layer_kernel(
    n,
    owner_ref, read_ref, src_ref, blk_ref, holder_ref, ctx_ref,
    q_ref, new_ref, kv_ref, pssm_ref, pool_ref, ossm_ref, conv_ref,
    x_ref, z_ref, dt_ref, bias_ref, alog_ref, gain_ref, cw_ref, cb_ref, wbc_ref,
    att_ref, mam_ref,
    q_all, pool_v, part_o, part_s, got_o, got_s,
    cand, piece, states,
    own, side, rightward, leftward, to_right, to_left, shared,
    q0_v, new_v, x_v, z_v, dt_v, bias_v, alog_v, gain_v, cw_v, cb_v, wbc_v,
    pad, sig, bc_mine, bc_theirs, spread, step_buf, push_buf, scan_buf,
    load_sems, own_sems, st_send, st_recv, p_send, p_recv, q_send, q_recv,
    ch_send, ch_recv, bc_send, bc_recv,
):
    me = lax.axis_index("replica")
    core = lax.axis_index("channel")
    line, half = me // 2, lax.rem(me, 2)
    length = n // 2
    last = length - 1
    partner = line * 2 + 1 - half
    owner = owner_ref[0]
    owner_line = owner // 2
    reading = read_ref[0] > 0
    states_n, channels = alog_v.shape
    new_len = q0_v.shape[0]
    heads = new_v.shape[2] // (2 * HD)
    rows = Q_PER_KV * new_len
    chunks, _, width = side.shape
    piece_w = cand.shape[2]
    per = width // piece_w
    wide = channels // width
    blocks_listed = src_ref.shape[0]

    barrier = pltpu.get_barrier_semaphore()
    for s in range(1, n):
        pl.semaphore_signal(
            barrier, inc=1, device_id={"replica": lax.rem(me + s, n)}, device_id_type=MESH
        )
    pl.semaphore_signal(barrier, inc=1, device_id={"channel": 1 - core}, device_id_type=MESH)

    loads = []

    def load(source, target):
        copy = pltpu.make_async_copy(source, target, load_sems.at[len(loads)])
        copy.start()
        loads.append(copy)
        return copy

    load_q = load(q_ref.at[0, 1], q_all.at[me])
    load_kv = load(kv_ref, own.at[:, pl.ds(1, chunks - 1)])
    load_ssm = []
    per_half = wide // 2
    for g in range(wide):
        load_ssm.append(
            load(
                pssm_ref.at[0, :, pl.ds(g * width, width)],
                own.at[g // per_half, 0, pl.ds(g % per_half * states_n, states_n)],
            )
        )
    mine = pl.ds(pl.multiple_of(me * piece_w, piece_w), piece_w)
    load_cand = [
        load(ossm_ref.at[0, :, mine], cand.at[me, pl.ds(0, states_n)]),
        load(conv_ref.at[:, mine], cand.at[me, pl.ds(states_n, 8)]),
    ]
    load_pool = load(pool_ref.at[0], pool_v)
    load_conv = [load(x_ref.at[0], x_v), load(cw_ref, cw_v), load(cb_ref, cb_v), load(wbc_ref, wbc_v)]
    load_scan = [
        load(dt_ref.at[0], dt_v), load(z_ref.at[0], z_v), load(bias_ref, bias_v),
        load(alog_ref, alog_v), load(gain_ref, gain_v),
    ]
    load_att = [load(q_ref.at[0, 0], q0_v), load(new_ref.at[0], new_v)]

    def remote(source, target, send_sem, recv_sem, peer):
        return pltpu.make_async_remote_copy(
            src_ref=source, dst_ref=target, send_sem=send_sem, recv_sem=recv_sem,
            device_id={"replica": peer}, device_id_type=MESH,
        )

    def peer_of(s):
        return lax.rem(me + s, n)

    load_q.wait()
    pl.semaphore_wait(barrier, n)

    def q_right(s):
        item = q_all.at[(line - s) * 2 + half]
        return remote(item, item, q_send.at[0, s], q_recv.at[0, s], lax.rem(me + 2, n))

    def q_left(s):
        item = q_all.at[(line + s) * 2 + half]
        return remote(item, item, q_send.at[1, s], q_recv.at[1, s], lax.rem(me + n - 2, n))

    def q_from_left(s):
        item = q_all.at[(line - s) * 2 + half]
        return remote(item, item, q_send.at[0, s - 1], q_recv.at[0, s - 1], partner)

    def q_from_right(s):
        item = q_all.at[(line + s) * 2 + half]
        return remote(item, item, q_send.at[1, s - 1], q_recv.at[1, s - 1], partner)

    def q_over(s):
        item = q_all.at[(line + s) * 2 + half]
        index = length - 1 + s
        return remote(item, item, q_send.at[2, index], q_recv.at[2, index], partner)

    @pl.when(line < last)
    def _():
        q_right(0).start()

    @pl.when(line > 0)
    def _():
        q_left(0).start()

    q_over(0).start()

    def state_first(kind, s):
        peer = peer_of(s)
        cols = pl.ds(pl.multiple_of(peer * piece_w, piece_w), piece_w)
        if kind == 0:
            source, target = ossm_ref.at[0, :, cols], cand.at[me, pl.ds(0, states_n)]
        else:
            source, target = conv_ref.at[:, cols], cand.at[me, pl.ds(states_n, 8)]
        return remote(source, target, st_send.at[kind, s], st_recv.at[kind, s], peer)

    def state_second(s):
        peer = peer_of(s)
        return remote(piece.at[peer], states.at[me], st_send.at[2, s], st_recv.at[2, s], peer)

    for s in range(1, n):
        state_first(0, s).start()
        state_first(1, s).start()

    def chain(kind, c, source, target, peer):
        return remote(source, target, ch_send.at[kind, c], ch_recv.at[kind, c], peer)

    def side_copy(c):
        return chain(0, c, own.at[1 - half, c], side.at[c], partner)

    def right_copy(c):
        return chain(1, c, to_right.at[c], rightward.at[c], lax.rem(me + 2, n))

    def left_copy(c):
        return chain(2, c, to_left.at[c], leftward.at[c], lax.rem(me + n - 2, n))

    def final_copy(c):
        return chain(3, c, shared.at[half, c], shared.at[half, c], partner)

    def here(c):
        return jnp.where(owner == me, own[half, c], side[c])

    near, far = jnp.minimum(line, last - line), jnp.maximum(line, last - line)

    def spread_step(t):
        if t + 1 < chunks:
            side_copy(t + 1).start()
        c_near, c_right, c_left, c_far = t - near, t - line, t - (last - line), t - far

        @pl.when((c_near >= 0) & (c_near < chunks))
        def _():
            side_copy(c_near).wait_recv()

        @pl.when((c_right >= 0) & (c_right < chunks))
        def _():
            @pl.when(line > 0)
            def _():
                right_copy(c_right).wait_recv()

            @pl.when(line < last)
            def _():
                to_right[c_right] = jnp.where(owner_line == line, here(c_right), rightward[c_right])
                right_copy(c_right).start()

        @pl.when((c_left >= 0) & (c_left < chunks))
        def _():
            @pl.when(line < last)
            def _():
                left_copy(c_left).wait_recv()

            @pl.when(line > 0)
            def _():
                to_left[c_left] = jnp.where(owner_line == line, here(c_left), leftward[c_left])
                left_copy(c_left).start()

        @pl.when((c_far >= 0) & (c_far < chunks))
        def _():
            shared[half, c_far] = jnp.where(
                owner_line == line,
                here(c_far),
                jnp.where(owner_line < line, rightward[c_far], leftward[c_far]),
            )
            final_copy(c_far).start()

    load_kv.wait()
    for copy in load_ssm:
        copy.wait()
    side_copy(0).start()

    for copy in load_cand:
        copy.wait()
    for s in range(1, n):
        state_first(0, s).wait_recv()
        state_first(1, s).wait_recv()
    conv_row = lax.broadcasted_iota(jnp.int32, (8, piece_w), 0)
    shared_conv = cand[owner, states_n:].astype(jnp.float32)
    for d in range(n):
        holder = holder_ref[d]
        piece[d, :states_n] = cand[holder, :states_n]
        stored_conv = cand[holder, states_n:].astype(jnp.float32)
        piece[d, states_n:] = jnp.where(conv_row < 3, stored_conv, shared_conv).astype(piece.dtype)
    for s in range(1, n):
        state_second(s).start()
    states[me] = piece[me]

    def query_rows(load_piece, head):
        return jnp.concatenate(
            [load_piece((head * Q_PER_KV + g) * HD) for g in range(Q_PER_KV)], axis=0
        )

    def key_cols(head):
        return slice(2 * head * HD, (2 * head + 1) * HD)

    def value_cols(head):
        return slice((2 * head + 1) * HD, (2 * head + 2) * HD)

    def partial(d, out_o, out_s):
        block = jnp.int32(0)
        for j in range(blocks_listed):
            block = block + jnp.where(src_ref[j, d] == me, blk_ref[j, d], 0)
        for head in range(heads):
            query = query_rows(lambda at: q_all[d, :, at : at + HD], head)
            score = scores_of(pool_v[block, :, key_cols(head)], query)
            highest = jnp.max(score, axis=0, keepdims=True)
            weight = jnp.exp(score - highest)
            mixed = mix(pool_v[block, :, value_cols(head)], weight)
            out_o[head * HD : (head + 1) * HD] = mixed.astype(jnp.bfloat16)
            out_s[head : head + 1] = highest
            out_s[heads + head : heads + head + 1] = jnp.sum(weight, axis=0, keepdims=True)

    def part_copies(s):
        peer = peer_of(s)
        return (
            remote(part_o.at[peer], got_o.at[me], p_send.at[0, s], p_recv.at[0, s], peer),
            remote(part_s.at[peer], got_s.at[me], p_send.at[1, s], p_recv.at[1, s], peer),
        )

    def relay_unit(s):
        def go():
            @pl.when(line - s >= 0)
            def _():
                q_from_left(s).wait_recv()

                @pl.when(line < last)
                def _():
                    q_right(s).start()

                q_over(-s).start()

            @pl.when(line + s <= last)
            def _():
                q_from_right(s).wait_recv()

                @pl.when(line > 0)
                def _():
                    q_left(s).start()

                q_over(s).start()

        return go

    def gathered():
        for s in range(-last, length):
            @pl.when((line + s >= 0) & (line + s <= last))
            def _():
                q_over(s).wait_recv()

        load_pool.wait()

    def visit_unit(low, high):
        def go():
            if low == 1:
                gathered()
                partial(me, got_o.at[me], got_s.at[me])

            def body(s, carry):
                peer = peer_of(s)
                partial(peer, part_o.at[peer], part_s.at[peer])
                for copy in part_copies(s):
                    copy.start()
                return carry

            lax.fori_loop(low, high, body, 0)

        return go

    taps = cw_v.shape[0]
    base = 8 - (taps - 1)

    def lanes(i):
        return pl.ds(pl.multiple_of(i * width, width), width)

    def stored(i):
        parts = [states[i * per + k].astype(jnp.float32) for k in range(per)]
        return parts[0] if per == 1 else jnp.concatenate(parts, axis=1)

    def bc_copy():
        return pltpu.make_async_remote_copy(
            src_ref=bc_mine, dst_ref=bc_theirs, send_sem=bc_send.at[0], recv_sem=bc_recv.at[0],
            device_id={"channel": 1 - core}, device_id_type=MESH,
        )

    def signal_unit(low, high):
        def go():
            if low == 0:
                for s in range(1, n):
                    state_second(s).wait_recv()
                for copy in load_conv:
                    copy.wait()
                bc_mine[...] = jnp.zeros_like(bc_mine)

            def body(i, carry):
                held = stored(i)[states_n:]
                pad[0, base:8] = jnp.where(reading, held[taps - 1 : 2 * taps - 2], 0.0)
                pad[1, base:8] = held[: taps - 1]
                both = []
                for r in range(2):
                    pad[r, 8 : 8 + new_len] = x_v[r, :, lanes(i)].astype(jnp.float32)
                    total = cb_v[:, lanes(i)] + cw_v[0:1, lanes(i)] * pad[r, base : base + new_len]
                    for k in range(1, taps):
                        total = total + cw_v[k : k + 1, lanes(i)] * pad[r, base + k : base + k + new_len]
                    signal = total * jax.nn.sigmoid(total)
                    sig[r, :, lanes(i)] = signal
                    both.append(signal.astype(jnp.bfloat16))
                bc_mine[:, : 2 * new_len] += lax.dot_general(
                    wbc_v[:, lanes(i)], jnp.concatenate(both, axis=0), (((1,), (1,)), ((), ())),
                    preferred_element_type=jnp.float32,
                )
                return carry

            lax.fori_loop(low, high, body, 0)
            if high == wide:
                bc_copy().start()

        return go

    def scan_unit(low, high):
        def go():
            if low == 0:
                bc_copy().wait_recv()
                total = bc_mine[...] + bc_theirs[...]
                for r in range(2):
                    for t in range(new_len):
                        at = r * new_len + t
                        spread[r, t] = jnp.broadcast_to(total[:, at : at + 1], spread.shape[2:])
                for copy in load_scan:
                    copy.wait()
                final_copy(0).wait_recv()

            def body(i, carry):
                decay = -jnp.exp(alog_v[:, lanes(i)])
                for r in range(2):
                    x = dt_v[r, :, lanes(i)].astype(jnp.float32) + bias_v[:, lanes(i)]
                    step = jnp.maximum(x, 0.0) + jnp.log1p(jnp.exp(-jnp.abs(x)))
                    step_buf[r] = step
                    push_buf[r] = step * sig[r, :, lanes(i)]
                group = pl.ds(pl.multiple_of(lax.rem(i, per_half) * states_n, states_n), states_n)
                first = shared[i // per_half, 0, group].astype(jnp.float32)
                hidden = [jnp.where(reading, first, 0.0), stored(i)[:states_n]]
                tiles = width // HD
                for t in range(new_len):
                    for r in range(2):
                        now = jnp.broadcast_to(step_buf[r, t : t + 1], (states_n, width))
                        push = jnp.broadcast_to(push_buf[r, t : t + 1], (states_n, width))
                        both = spread[r, t]
                        gain = jnp.concatenate([both[:states_n]] * tiles, axis=1)
                        read = jnp.concatenate([both[states_n:]] * tiles, axis=1)
                        hidden[r] = jnp.exp(now * decay) * hidden[r] + gain * push
                        scan_buf[r, t : t + 1] = jnp.sum(read * hidden[r], axis=0, keepdims=True)
                for r in range(2):
                    z = z_v[r, :, lanes(i)].astype(jnp.float32)
                    full = scan_buf[r] + gain_v[:, lanes(i)] * sig[r, :, lanes(i)]
                    mam_ref[0, r, :, lanes(i)] = (full * (z * jax.nn.sigmoid(z))).astype(mam_ref.dtype)
                return carry

            lax.fori_loop(low, high, body, 0)

        return go

    visits = [1 + (n - 1) * k // 2 for k in range(3)]
    units = [relay_unit(s) for s in range(1, length)]
    units += [visit_unit(low, high) for low, high in zip(visits[:-1], visits[1:])]
    units += [signal_unit(0, wide // 2), signal_unit(wide // 2, wide)]
    units += [scan_unit(k * wide // 4, (k + 1) * wide // 4) for k in range(4)]
    steps = chunks + length - 1
    done = 0
    for t in range(steps):
        spread_step(t)
        until = (t + 1) * len(units) // steps
        for unit in units[done:until]:
            unit()
        done = until

    for c in range(1, chunks):
        final_copy(c).wait_recv()
    for copy in load_att:
        copy.wait()

    def causal(score):
        key = lax.broadcasted_iota(jnp.int32, score.shape, 0)
        time = lax.rem(lax.broadcasted_iota(jnp.int32, score.shape, 1), new_len)
        return jnp.where(time >= key, score, -jnp.inf)

    def put(request, head, mixed, total):
        result = (mixed / total).T.astype(att_ref.dtype)
        for g in range(Q_PER_KV):
            at = (head * Q_PER_KV + g) * HD
            att_ref[0, request, :, at : at + HD] = result[g * new_len : (g + 1) * new_len]

    for head in range(heads):
        query = query_rows(lambda at: q0_v[:, at : at + HD], head)
        fresh = causal(scores_of(new_v[0, :, key_cols(head)], query))
        highest = jnp.max(fresh, axis=0, keepdims=True)
        scores = []
        for h in range(2):
            keys = shared[h, 1:, :, key_cols(head)].reshape(-1, HD)
            score = jnp.where(reading, scores_of(keys, query), -jnp.inf)
            highest = jnp.maximum(highest, jnp.max(score, axis=0, keepdims=True))
            scores.append(score)
        weight = jnp.exp(fresh - highest)
        total = jnp.sum(weight, axis=0, keepdims=True)
        mixed = mix(new_v[0, :, value_cols(head)], weight)
        for h in range(2):
            weight = jnp.exp(scores[h] - highest)
            total = total + jnp.sum(weight, axis=0, keepdims=True)
            mixed = mixed + mix(shared[h, 1:, :, value_cols(head)].reshape(-1, HD), weight)
        put(0, head, mixed, total)

    for s in range(1, n):
        for copy in part_copies(s):
            copy.wait_recv()
    live = ctx_ref[0]
    for head in range(heads):
        query = query_rows(lambda at: q_all[me, :, at : at + HD], head)
        fresh = causal(scores_of(new_v[1, :, key_cols(head)], query))
        highest = jnp.max(fresh, axis=0, keepdims=True)
        tops = []
        for j in range(blocks_listed):
            top = jnp.where(j < live, got_s[src_ref[j, me], head : head + 1], -jnp.inf)
            tops.append(top)
            highest = jnp.maximum(highest, top)
        weight = jnp.exp(fresh - highest)
        total = jnp.sum(weight, axis=0, keepdims=True)
        mixed = mix(new_v[1, :, value_cols(head)], weight)
        for j in range(blocks_listed):
            source = src_ref[j, me]
            scale = jnp.exp(tops[j] - highest)
            total = total + scale * got_s[source, heads + head : heads + head + 1]
            mixed = mixed + scale * got_o[source, head * HD : (head + 1) * HD].astype(jnp.float32)
        put(1, head, mixed, total)

    for s in range(1, n):
        state_first(0, s).wait_send()
        state_first(1, s).wait_send()
        state_second(s).wait_send()
        for copy in part_copies(s):
            copy.wait_send()
    bc_copy().wait_send()
    q_over(0).wait_send()

    @pl.when(line < last)
    def _():
        q_right(0).wait_send()

    @pl.when(line > 0)
    def _():
        q_left(0).wait_send()

    for s in range(1, length):
        @pl.when(line - s >= 0)
        def _():
            q_over(-s).wait_send()

            @pl.when(line < last)
            def _():
                q_right(s).wait_send()

        @pl.when(line + s <= last)
        def _():
            q_over(s).wait_send()

            @pl.when(line > 0)
            def _():
                q_left(s).wait_send()

    for c in range(chunks):
        side_copy(c).wait_send()
        final_copy(c).wait_send()

        @pl.when(line < last)
        def _():
            right_copy(c).wait_send()

        @pl.when(line > 0)
        def _():
            left_copy(c).wait_send()


def local(
    queries,
    new_kv,
    cached_lookup_pairs,
    prefix_ssm,
    prefix_conv,
    pool_kv,
    pool_ssm,
    pool_conv,
    owner_id,
    readers,
    restore_src,
    restore_blk,
    state_src,
    ctx_blocks,
    mamba_x,
    mamba_z,
    mamba_dt,
    dt_bias,
    a_log,
    bypass_gain,
    conv_w,
    conv_b,
    w_bc,
):
    n = restore_src.shape[0]
    half_n = n // 2
    _, length, width = cached_lookup_pairs.shape
    _, states, channels = pool_ssm.shape
    _, _, new_len, q_width = queries.shape
    blocks, block_len = pool_kv.shape[1:3]
    part = length // 2 // KV_CHUNKS
    taps = conv_w.shape[0]
    assert part == channels // 2 // width * states and 2 * (taps - 1) <= 8
    kv = cached_lookup_pairs.reshape(2, KV_CHUNKS, part, width)
    fill = jnp.zeros((8 - 2 * (taps - 1), channels), pool_conv.dtype)
    conv = jnp.concatenate([pool_conv[0], prefix_conv[0], fill], axis=0)
    piece = (n, states + 8, channels // n)
    heads = width // (2 * HD)
    rows = Q_PER_KV * new_len
    chunks = KV_CHUNKS + 1
    bf16, f32 = jnp.bfloat16, jnp.float32
    smem = pl.BlockSpec(memory_space=pltpu.SMEM)
    any_spec = pl.BlockSpec(memory_space=pl.ANY)
    vmem = pl.BlockSpec(memory_space=pltpu.VMEM)
    stream = pltpu.VMEM((chunks, part, width), bf16)
    both = pltpu.VMEM((2, chunks, part, width), bf16)
    dma = pltpu.SemaphoreType.DMA
    return pl.pallas_call(
        lambda *refs: layer_kernel(n, *refs),
        in_specs=[smem] * 6 + [any_spec] * 16,
        out_specs=[vmem] * 2,
        out_shape=[
            jax.ShapeDtypeStruct((1, 2, new_len, q_width), bf16),
            jax.ShapeDtypeStruct((1, 2, new_len, channels), bf16),
        ],
        scratch_shapes=[
            pltpu.VMEM((n, new_len, q_width), bf16),
            pltpu.VMEM((blocks, block_len, width), bf16),
            pltpu.VMEM((n, heads * HD, rows), bf16),
            pltpu.VMEM((n, 8, rows), f32),
            pltpu.VMEM((n, heads * HD, rows), bf16),
            pltpu.VMEM((n, 8, rows), f32),
            pltpu.VMEM(piece, bf16),
            pltpu.VMEM(piece, bf16),
            pltpu.VMEM(piece, bf16),
            both,
        ]
        + [stream] * 5
        + [
            both,
            pltpu.VMEM((new_len, q_width), bf16),
            pltpu.VMEM((2, new_len, width), bf16),
        ]
        + [pltpu.VMEM((2, new_len, channels), bf16)] * 3
        + [
            pltpu.VMEM((1, channels), f32),
            pltpu.VMEM((states, channels), f32),
            pltpu.VMEM((1, channels), f32),
            pltpu.VMEM((taps, channels), f32),
            pltpu.VMEM((1, channels), f32),
            pltpu.VMEM((2 * states, channels), bf16),
            pltpu.VMEM((2, 8 + new_len, width), f32),
            pltpu.VMEM((2, new_len, channels), f32),
            pltpu.VMEM((2 * states, 128), f32),
            pltpu.VMEM((2 * states, 128), f32),
            pltpu.VMEM((2, new_len, 2 * states, HD), f32),
            pltpu.VMEM((2, new_len, width), f32),
            pltpu.VMEM((2, new_len, width), f32),
            pltpu.VMEM((2, new_len, width), f32),
            dma((32,)),
            dma((1,)),
            dma((3, n)),
            dma((3, n)),
            dma((2, n)),
            dma((2, n)),
            dma((3, n)),
            dma((3, n)),
            dma((4, chunks)),
            dma((4, chunks)),
            dma((1,)),
            dma((1,)),
        ],
        compiler_params=pltpu.CompilerParams(collective_id=0, has_side_effects=True),
        name="layer",
    )(
        owner_id, readers, jnp.swapaxes(restore_src, 0, 1), jnp.swapaxes(restore_blk, 0, 1), state_src, ctx_blocks,
        queries, new_kv, kv, prefix_ssm, pool_kv, pool_ssm, conv,
        mamba_x, mamba_z, mamba_dt, dt_bias[None], a_log, bypass_gain[None], conv_w, conv_b[None],
        jnp.swapaxes(w_bc, 0, 1),
    )


def placed_specs():
    return (
        P(("groups", "replica"), None, None, "channel"),
        P(("groups", "replica"), None, None, "channel"),
        P(("groups", "replica"), None, "channel"),
        P(("groups", "replica"), None, "channel"),
        P(("groups", "replica"), None, "channel"),
        P(("groups", "replica"), None, None, "channel"),
        P(("groups", "replica"), None, "channel"),
        P(("groups", "replica"), None, "channel"),
        P("groups"),
        P(("groups", "replica")),
        P("groups", None),
        P("groups", None),
        P("groups"),
        P(("groups", "replica")),
        P(("groups", "replica"), None, None, "channel"),
        P(("groups", "replica"), None, None, "channel"),
        P(("groups", "replica"), None, None, "channel"),
        P("channel"),
        P(None, "channel"),
        P("channel"),
        P(None, "channel"),
        P("channel"),
        P("channel", None),
    )


def solution(mesh):
    return jax.shard_map(
        local,
        mesh=mesh,
        in_specs=placed_specs(),
        out_specs=(
            P(("groups", "replica"), None, None, "channel"),
            P(("groups", "replica"), None, None, "channel"),
        ),
        check_vma=False,
    )
```

```python
import jax
import jax.numpy as jnp
from jax import lax
from jax.experimental import pallas as pl
from jax.experimental.pallas import tpu as pltpu
from jax.sharding import PartitionSpec as P

HD = 128
Q_PER_KV = 8
KV_CHUNKS = 16
SKEW = 4
AHEAD = 6
RELAYS = (0.02, 0.3)
OVERS = (0.34, 0.6)
KEEPS = (0.65, 0.95)
SIGNALS = (0.2, 0.36)
SCANS = (0.42, 0.95)
OUT_OF_REACH = -1e30
MESH = pl.DeviceIdType.MESH


def scores_of(keys, query):
    contract = (((1,), (1,)), ((), ()))
    return lax.dot_general(keys, query, contract, preferred_element_type=jnp.float32) * (HD ** (-0.5))


def mix(values, weight):
    contract = (((0,), (0,)), ((), ()))
    return lax.dot_general(values, weight.astype(jnp.bfloat16), contract, preferred_element_type=jnp.float32)


def layer_kernel(
    n,
    owner_any, read_any, src_any, blk_any, holder_any, ctx_any,
    q_ref, new_ref, kv_ref, pssm_ref, pool_ref, ossm_ref, oconv_ref, pconv_ref,
    x_ref, z_ref, dt_ref, bias_ref, alog_ref, gain_ref, cw_ref, cb_ref, wbc_ref,
    att_ref, mam_ref,
    owner_ref, read_ref, src_ref, blk_ref, holder_ref, ctx_ref, oconv_v, pconv_v, conv_f, conv_ref,
    q_all, pool_v, over_o, over_s, side_o, side_s, keep_o, keep_s, got_o, got_s,
    cand, piece, states,
    own, side, rightward, leftward, to_right, to_left, shared,
    q0_v, new_v, x_v, z_v, dt_v, bias_v, alog_v, gain_v, cw_v, cb_v, wbc_v,
    pad, sig, bc_mine, bc_theirs, spread, step_buf, push_buf, scan_buf,
    load_sems, st_send, st_recv, p_send, p_recv, q_send, q_recv,
    ch_send, ch_recv, bc_send, bc_recv,
):
    me = lax.axis_index("replica")
    core = lax.axis_index("channel")
    line, half = me // 2, lax.rem(me, 2)
    length = n // 2
    last = last_line = length - 1
    partner = line * 2 + 1 - half
    states_n, channels = alog_v.shape
    new_len = q0_v.shape[0]
    heads = new_v.shape[2] // (2 * HD)
    rows = Q_PER_KV * new_len
    chunks, part, width = side.shape
    piece_w = cand.shape[2]
    per = width // piece_w
    wide = channels // width
    per_half = wide // 2
    lead = per_half * states_n // part
    per_part = part // states_n
    taps = cw_v.shape[0]
    blocks_listed = src_ref.shape[0]

    barrier = pltpu.get_barrier_semaphore()
    for s in range(1, n):
        pl.semaphore_signal(
            barrier, inc=1, device_id={"replica": lax.rem(me + s, n)}, device_id_type=MESH
        )
    pl.semaphore_signal(barrier, inc=1, device_id={"channel": 1 - core}, device_id_type=MESH)

    loads = []

    def load(source, target):
        copy = pltpu.make_async_copy(source, target, load_sems.at[len(loads)])
        copy.start()
        loads.append(copy)
        return copy

    load_q = load(q_ref.at[0, 1], q_all.at[me])
    load_rows = [load(oconv_ref.at[0], oconv_v), load(pconv_ref.at[0], pconv_v)]
    load_scalars = [
        load(owner_any, owner_ref), load(read_any, read_ref), load(src_any, src_ref),
        load(blk_any, blk_ref), load(holder_any, holder_ref), load(ctx_any, ctx_ref),
    ]
    load_kv = load(kv_ref, own.at[:, pl.ds(lead, chunks - lead)])
    load_ssm = []
    for g in range(wide):
        load_ssm.append(
            load(
                pssm_ref.at[0, :, pl.ds(g * width, width)],
                own.at[
                    g // per_half,
                    g % per_half * states_n // part,
                    pl.ds(g % per_half * states_n % part, states_n),
                ],
            )
        )
    mine = pl.ds(pl.multiple_of(me * piece_w, piece_w), piece_w)
    load_cand = load(ossm_ref.at[0, :, mine], cand.at[me, pl.ds(0, states_n)])
    load_pool = load(pool_ref.at[0], pool_v)
    load_conv = [load(x_ref.at[0], x_v), load(cw_ref, cw_v), load(cb_ref, cb_v), load(wbc_ref, wbc_v)]
    load_scan = [
        load(dt_ref.at[0], dt_v), load(z_ref.at[0], z_v), load(bias_ref, bias_v),
        load(alog_ref, alog_v), load(gain_ref, gain_v),
    ]
    load_att = [load(q_ref.at[0, 0], q0_v), load(new_ref.at[0], new_v)]

    def remote(source, target, send_sem, recv_sem, peer):
        return pltpu.make_async_remote_copy(
            src_ref=source, dst_ref=target, send_sem=send_sem, recv_sem=recv_sem,
            device_id={"replica": peer}, device_id_type=MESH,
        )

    def peer_of(s):
        return lax.rem(me + s, n)

    for copy in load_rows + load_scalars:
        copy.wait()
    conv_f[...] = jnp.zeros_like(conv_f)
    conv_f[: taps - 1] = oconv_v[...].astype(jnp.float32)
    conv_f[taps - 1 : 2 * taps - 2] = pconv_v[...].astype(jnp.float32)
    conv_f[2 * taps - 2 : 2 * taps - 1] = jnp.full((1, channels), ctx_ref[0].astype(jnp.float32))
    conv_ref[...] = conv_f[...].astype(conv_ref.dtype)
    cand[me, states_n:] = conv_ref[:, mine]
    owner = owner_ref[0]
    owner_line = owner // 2
    reading = read_ref[0] > 0
    load_q.wait()
    pl.semaphore_wait(barrier, n)

    def q_item(s, kind):
        return q_all.at[(line + s) * 2 + (half if kind == 0 else 1 - half)]

    def q_over():
        item = q_item(0, 0)
        return remote(item, item, q_send.at[4, 0], q_recv.at[4, 0], partner)

    def q_right(s, kind):
        item = q_item(-s, kind)
        return remote(item, item, q_send.at[kind, s], q_recv.at[kind, s], lax.rem(me + 2, n))

    def q_left(s, kind):
        item = q_item(s, kind)
        return remote(item, item, q_send.at[2 + kind, s], q_recv.at[2 + kind, s], lax.rem(me + n - 2, n))

    def q_arrival(s, kind, leftward_bound):
        item = q_item(s if leftward_bound else -s, kind)
        row = kind + (2 if leftward_bound else 0)
        return remote(item, item, q_send.at[row, s - 1], q_recv.at[row, s - 1], partner)

    def q_start(kind):
        @pl.when(line < last)
        def _():
            q_right(0, kind).start()

        @pl.when(line > 0)
        def _():
            q_left(0, kind).start()

    q_over().start()
    q_start(0)

    def state_first(kind, s):
        peer = peer_of(s)
        cols = pl.ds(pl.multiple_of(peer * piece_w, piece_w), piece_w)
        if kind == 0:
            source, target = ossm_ref.at[0, :, cols], cand.at[me, pl.ds(0, states_n)]
        else:
            source, target = conv_ref.at[:, cols], cand.at[me, pl.ds(states_n, 8)]
        return remote(source, target, st_send.at[kind, s], st_recv.at[kind, s], peer)

    def state_second(s):
        peer = peer_of(s)
        return remote(piece.at[peer], states.at[me], st_send.at[2, s], st_recv.at[2, s], peer)

    for s in range(1, n):
        state_first(0, s).start()
        state_first(1, s).start()

    def chain(kind, c, source, target, peer):
        return remote(source, target, ch_send.at[kind, c], ch_recv.at[kind, c], peer)

    def side_copy(c):
        return chain(0, c, own.at[1 - half, c], side.at[c], partner)

    def right_copy(c):
        return chain(1, c, to_right.at[c], rightward.at[c], lax.rem(me + 2, n))

    def left_copy(c):
        return chain(2, c, to_left.at[c], leftward.at[c], lax.rem(me + n - 2, n))

    def final_copy(c):
        return chain(3, c, shared.at[half, c], shared.at[half, c], partner)

    def here(c):
        return jnp.where(owner == me, own[half, c], side[c])

    near, far = jnp.minimum(line, last - line), jnp.maximum(line, last - line)

    def spread_step(t):
        if t + AHEAD < chunks:
            side_copy(t + AHEAD).start()
        c_near, c_far = t - SKEW * near, t - SKEW * far
        c_right, c_left = t - SKEW * line, t - SKEW * (last - line)

        @pl.when((c_near >= 0) & (c_near < chunks))
        def _():
            side_copy(c_near).wait_recv()

        @pl.when((c_right >= 0) & (c_right < chunks))
        def _():
            @pl.when(line > 0)
            def _():
                right_copy(c_right).wait_recv()

            @pl.when(line < last)
            def _():
                to_right[c_right] = jnp.where(owner_line == line, here(c_right), rightward[c_right])
                right_copy(c_right).start()

        @pl.when((c_left >= 0) & (c_left < chunks))
        def _():
            @pl.when(line < last)
            def _():
                left_copy(c_left).wait_recv()

            @pl.when(line > 0)
            def _():
                to_left[c_left] = jnp.where(owner_line == line, here(c_left), leftward[c_left])
                left_copy(c_left).start()

        @pl.when((c_far >= 0) & (c_far < chunks))
        def _():
            shared[half, c_far] = jnp.where(
                owner_line == line,
                here(c_far),
                jnp.where(owner_line < line, rightward[c_far], leftward[c_far]),
            )
            final_copy(c_far).start()

    load_kv.wait()
    for copy in load_ssm:
        copy.wait()
    for c in range(AHEAD):
        side_copy(c).start()

    def state_unit():
        load_cand.wait()
        for s in range(1, n):
            state_first(0, s).wait_recv()
            state_first(1, s).wait_recv()
        conv_row = lax.broadcasted_iota(jnp.int32, (8, piece_w), 0)
        shared_conv = cand[owner, states_n:].astype(jnp.float32)
        for d in range(n):
            holder = holder_ref[d]
            piece[d, :states_n] = cand[holder, :states_n]
            stored_conv = cand[holder, states_n:].astype(jnp.float32)
            merged = jnp.where(conv_row < taps - 1, stored_conv, shared_conv)
            piece[d, states_n:] = merged.astype(piece.dtype)
        for s in range(1, n):
            state_second(s).start()
        states[me] = piece[me]

    def query_rows(load_piece, head):
        return jnp.concatenate(
            [load_piece((head * Q_PER_KV + g) * HD) for g in range(Q_PER_KV)], axis=0
        )

    def key_cols(head):
        return slice(2 * head * HD, (2 * head + 1) * HD)

    def value_cols(head):
        return slice((2 * head + 1) * HD, (2 * head + 2) * HD)

    def partial(d):
        block, slot = jnp.int32(0), jnp.int32(blocks_listed * n)
        for j in range(blocks_listed):
            listed = src_ref[j, d] == me
            block = block + jnp.where(listed, blk_ref[j, d], 0)
            slot = jnp.where(listed, j, slot)
        held = cand[d, states_n:, :HD].astype(jnp.float32)[2 * taps - 2 : 2 * taps - 1]
        held = jnp.concatenate([held] * (rows // HD), axis=1)
        live = slot.astype(jnp.float32) < held
        results = []
        for head in range(heads):
            query = query_rows(lambda at: q_all[d, :, at : at + HD], head)
            score = scores_of(pool_v[block, :, key_cols(head)], query)
            highest = jnp.max(score, axis=0, keepdims=True)
            weight = jnp.exp(score - highest)
            mixed = mix(pool_v[block, :, value_cols(head)], weight)
            total = jnp.sum(weight, axis=0, keepdims=True)
            results.append((mixed, jnp.where(live, highest, OUT_OF_REACH), total))
        return results

    def store(out_o, out_s, head, mixed, highest, total):
        out_o[head * HD : (head + 1) * HD] = mixed.astype(jnp.bfloat16)
        out_s[head : head + 1] = highest
        out_s[heads + head : heads + head + 1] = total

    def line_of(s):
        return lax.rem(line + s, length)

    def over_copies(s):
        at = line_of(s)
        return (
            remote(over_o.at[at], side_o.at[at], p_send.at[0, s], p_recv.at[0, s], partner),
            remote(over_s.at[at], side_s.at[at], p_send.at[1, s], p_recv.at[1, s], partner),
        )

    def keep_copies(s):
        at = line_of(s)
        peer = at * 2 + half
        return (
            remote(keep_o.at[at], got_o.at[line], p_send.at[2, s], p_recv.at[2, s], peer),
            remote(keep_s.at[at], got_s.at[line], p_send.at[3, s], p_recv.at[3, s], peer),
        )

    def relay_unit(s):
        def go():
            if s == 0:
                q_over().wait_recv()
                q_start(1)
                return
            for kind in range(2):
                @pl.when(line - s >= 0)
                def _():
                    q_arrival(s, kind, False).wait_recv()

                    @pl.when(line < last)
                    def _():
                        q_right(s, kind).start()

                @pl.when(line + s <= last)
                def _():
                    q_arrival(s, kind, True).wait_recv()

                    @pl.when(line > 0)
                    def _():
                        q_left(s, kind).start()

        return go

    def over_unit(low, high):
        def go():
            if low == 0:
                load_pool.wait()

            def body(s, carry):
                at = line_of(s)
                for head, result in enumerate(partial(at * 2 + 1 - half)):
                    store(over_o.at[at], over_s.at[at], head, *result)
                for copy in over_copies(s):
                    copy.start()
                return carry

            lax.fori_loop(low, high, body, 0)

        return go

    def keep_row(s, out_o, out_s):
        at = line_of(s)
        results = partial(at * 2 + half)
        for copy in over_copies(s):
            copy.wait_recv()
        for head, (mixed, highest, total) in enumerate(results):
            theirs = side_s[at, head : head + 1]
            both = jnp.maximum(highest, theirs)
            ours, theirs = jnp.exp(highest - both), jnp.exp(theirs - both)
            mixed = ours * mixed + theirs * side_o[at, head * HD : (head + 1) * HD].astype(jnp.float32)
            total = ours * total + theirs * side_s[at, heads + head : heads + head + 1]
            store(out_o, out_s, head, mixed, both, total)

    def keep_unit(low, high):
        def go():
            def body(s, carry):
                at = line_of(s)
                keep_row(s, keep_o.at[at], keep_s.at[at])
                for copy in keep_copies(s):
                    copy.start()
                return carry

            lax.fori_loop(low, high, body, 0)

        return go

    def own_unit():
        keep_row(0, got_o.at[line], got_s.at[line])

    base = 8 - (taps - 1)

    def lanes(i):
        return pl.ds(pl.multiple_of(i * width, width), width)

    def stored(i):
        parts = [states[i * per + k].astype(jnp.float32) for k in range(per)]
        return parts[0] if per == 1 else jnp.concatenate(parts, axis=1)

    def bc_copy():
        return pltpu.make_async_remote_copy(
            src_ref=bc_mine, dst_ref=bc_theirs, send_sem=bc_send.at[0], recv_sem=bc_recv.at[0],
            device_id={"channel": 1 - core}, device_id_type=MESH,
        )

    def signal_unit(low, high):
        def go():
            if low == 0:
                for s in range(1, n):
                    state_second(s).wait_recv()
                for copy in load_conv:
                    copy.wait()
                bc_mine[...] = jnp.zeros_like(bc_mine)

            def body(i, carry):
                held = stored(i)[states_n:]
                pad[0, base:8] = jnp.where(reading, held[taps - 1 : 2 * taps - 2], 0.0)
                pad[1, base:8] = held[: taps - 1]
                both = []
                for r in range(2):
                    pad[r, 8 : 8 + new_len] = x_v[r, :, lanes(i)].astype(jnp.float32)
                    total = cb_v[:, lanes(i)] + cw_v[0:1, lanes(i)] * pad[r, base : base + new_len]
                    for k in range(1, taps):
                        total = total + cw_v[k : k + 1, lanes(i)] * pad[r, base + k : base + k + new_len]
                    signal = total * jax.nn.sigmoid(total)
                    sig[r, :, lanes(i)] = signal
                    both.append(signal.astype(jnp.bfloat16))
                bc_mine[:, : 2 * new_len] += lax.dot_general(
                    wbc_v[:, lanes(i)], jnp.concatenate(both, axis=0), (((1,), (1,)), ((), ())),
                    preferred_element_type=jnp.float32,
                )
                return carry

            lax.fori_loop(low, high, body, 0)
            if high == wide:
                bc_copy().start()

        return go

    def scan_unit(low, high):
        def go():
            if low == 0:
                bc_copy().wait_recv()
                total = bc_mine[...] + bc_theirs[...]
                for r in range(2):
                    for t in range(new_len):
                        at = r * new_len + t
                        spread[r, t] = jnp.broadcast_to(total[:, at : at + 1], spread.shape[2:])
                for copy in load_scan:
                    copy.wait()
                for c in range(lead):
                    final_copy(c).wait_recv()

            def body(i, carry):
                decay = -jnp.exp(alog_v[:, lanes(i)])
                for r in range(2):
                    x = dt_v[r, :, lanes(i)].astype(jnp.float32) + bias_v[:, lanes(i)]
                    step = jnp.maximum(x, 0.0) + jnp.log1p(jnp.exp(-jnp.abs(x)))
                    step_buf[r] = step
                    push_buf[r] = step * sig[r, :, lanes(i)]
                place = lax.rem(i, per_half)
                group = pl.ds(pl.multiple_of(lax.rem(place, per_part) * states_n, states_n), states_n)
                first = shared[i // per_half, place // per_part, group].astype(jnp.float32)
                hidden = [jnp.where(reading, first, 0.0), stored(i)[:states_n]]
                tiles = width // HD
                for t in range(new_len):
                    for r in range(2):
                        now = jnp.broadcast_to(step_buf[r, t : t + 1], (states_n, width))
                        push = jnp.broadcast_to(push_buf[r, t : t + 1], (states_n, width))
                        both = spread[r, t]
                        gain = jnp.concatenate([both[:states_n]] * tiles, axis=1)
                        read = jnp.concatenate([both[states_n:]] * tiles, axis=1)
                        hidden[r] = jnp.exp(now * decay) * hidden[r] + gain * push
                        scan_buf[r, t : t + 1] = jnp.sum(read * hidden[r], axis=0, keepdims=True)
                for r in range(2):
                    z = z_v[r, :, lanes(i)].astype(jnp.float32)
                    full = scan_buf[r] + gain_v[:, lanes(i)] * sig[r, :, lanes(i)]
                    mam_ref[0, r, :, lanes(i)] = (full * (z * jax.nn.sigmoid(z))).astype(mam_ref.dtype)
                return carry

            lax.fori_loop(low, high, body, 0)

        return go

    def spaced(span, units):
        gap = (span[1] - span[0]) / max(len(units) - 1, 1)
        return [(span[0] + gap * k, unit) for k, unit in enumerate(units)]

    def grouped(make, low, high, most):
        count = min(most, high - low)
        edges = [low + (high - low) * k // count for k in range(count + 1)]
        return [make(a, b) for a, b in zip(edges[:-1], edges[1:])]

    relays = [relay_unit(s) for s in range(length)]
    plan = spaced(RELAYS, relays[:2] + [state_unit] + relays[2:])
    plan += spaced(OVERS, grouped(over_unit, 0, length, 4))
    plan += spaced(KEEPS, grouped(keep_unit, 1, length, 3) + [own_unit])
    plan += spaced(SIGNALS, grouped(signal_unit, 0, wide, 2))
    steps = chunks + SKEW * last_line
    ready = (SKEW * last_line + lead + 1) / steps
    plan += spaced((max(SCANS[0], ready), max(SCANS[1], ready)), grouped(scan_unit, 0, wide, 8))
    plan.sort(key=lambda entry: entry[0])
    for t in range(steps):
        spread_step(t)
        while plan and plan[0][0] * steps <= t + 1:
            plan.pop(0)[1]()

    for c in range(lead, chunks):
        final_copy(c).wait_recv()
    for copy in load_att:
        copy.wait()

    def causal(score):
        key = lax.broadcasted_iota(jnp.int32, score.shape, 0)
        time = lax.rem(lax.broadcasted_iota(jnp.int32, score.shape, 1), new_len)
        return jnp.where(time >= key, score, -jnp.inf)

    def put(request, head, mixed, total):
        result = (mixed / total).T.astype(att_ref.dtype)
        for g in range(Q_PER_KV):
            at = (head * Q_PER_KV + g) * HD
            att_ref[0, request, :, at : at + HD] = result[g * new_len : (g + 1) * new_len]

    for head in range(heads):
        query = query_rows(lambda at: q0_v[:, at : at + HD], head)
        fresh = causal(scores_of(new_v[0, :, key_cols(head)], query))
        highest = jnp.max(fresh, axis=0, keepdims=True)
        scores = []
        for h in range(2):
            keys = shared[h, lead:, :, key_cols(head)].reshape(-1, HD)
            score = jnp.where(reading, scores_of(keys, query), -jnp.inf)
            highest = jnp.maximum(highest, jnp.max(score, axis=0, keepdims=True))
            scores.append(score)
        weight = jnp.exp(fresh - highest)
        total = jnp.sum(weight, axis=0, keepdims=True)
        mixed = mix(new_v[0, :, value_cols(head)], weight)
        for h in range(2):
            weight = jnp.exp(scores[h] - highest)
            total = total + jnp.sum(weight, axis=0, keepdims=True)
            mixed = mixed + mix(shared[h, lead:, :, value_cols(head)].reshape(-1, HD), weight)
        put(0, head, mixed, total)

    for s in range(1, length):
        for copy in keep_copies(s):
            copy.wait_recv()
    for head in range(heads):
        query = query_rows(lambda at: q_all[me, :, at : at + HD], head)
        fresh = causal(scores_of(new_v[1, :, key_cols(head)], query))
        highest = jnp.max(fresh, axis=0, keepdims=True)
        for at in range(length):
            highest = jnp.maximum(highest, got_s[at, head : head + 1])
        weight = jnp.exp(fresh - highest)
        total = jnp.sum(weight, axis=0, keepdims=True)
        mixed = mix(new_v[1, :, value_cols(head)], weight)
        for at in range(length):
            scale = jnp.exp(got_s[at, head : head + 1] - highest)
            total = total + scale * got_s[at, heads + head : heads + head + 1]
            mixed = mixed + scale * got_o[at, head * HD : (head + 1) * HD].astype(jnp.float32)
        put(1, head, mixed, total)

    for s in range(1, n):
        state_first(0, s).wait_send()
        state_first(1, s).wait_send()
        state_second(s).wait_send()
    bc_copy().wait_send()
    q_over().wait_send()
    for s in range(length):
        for copy in over_copies(s):
            copy.wait_send()
        if s > 0:
            for copy in keep_copies(s):
                copy.wait_send()
        for kind in range(2):
            @pl.when((line - s >= 0) & (line < last))
            def _():
                q_right(s, kind).wait_send()

            @pl.when((line + s <= last) & (line > 0))
            def _():
                q_left(s, kind).wait_send()

    for c in range(chunks):
        side_copy(c).wait_send()
        final_copy(c).wait_send()

        @pl.when(line < last)
        def _():
            right_copy(c).wait_send()

        @pl.when(line > 0)
        def _():
            left_copy(c).wait_send()


def local(
    queries,
    new_kv,
    cached_lookup_pairs,
    prefix_ssm,
    prefix_conv,
    pool_kv,
    pool_ssm,
    pool_conv,
    owner_id,
    readers,
    restore_src,
    restore_blk,
    state_src,
    ctx_blocks,
    mamba_x,
    mamba_z,
    mamba_dt,
    dt_bias,
    a_log,
    bypass_gain,
    conv_w,
    conv_b,
    w_bc,
):
    n = restore_src.shape[0]
    half_n = n // 2
    _, length, width = cached_lookup_pairs.shape
    _, states, channels = pool_ssm.shape
    _, _, new_len, q_width = queries.shape
    blocks, block_len = pool_kv.shape[1:3]
    part = length // 2 // KV_CHUNKS
    taps = conv_w.shape[0]
    lead = channels // 2 // width * states // part
    assert lead * part == channels // 2 // width * states and part % states == 0 and 2 * (taps - 1) < 8
    kv = cached_lookup_pairs.reshape(2, KV_CHUNKS, part, width)
    piece = (n, states + 8, channels // n)
    heads = width // (2 * HD)
    rows = Q_PER_KV * new_len
    chunks = KV_CHUNKS + lead
    bf16, f32 = jnp.bfloat16, jnp.float32
    any_spec = pl.BlockSpec(memory_space=pl.ANY)
    vmem = pl.BlockSpec(memory_space=pltpu.VMEM)
    stream = pltpu.VMEM((chunks, part, width), bf16)
    both = pltpu.VMEM((2, chunks, part, width), bf16)
    dma = pltpu.SemaphoreType.DMA
    return pl.pallas_call(
        lambda *refs: layer_kernel(n, *refs),
        in_specs=[any_spec] * 23,
        out_specs=[vmem] * 2,
        out_shape=[
            jax.ShapeDtypeStruct((1, 2, new_len, q_width), bf16),
            jax.ShapeDtypeStruct((1, 2, new_len, channels), bf16),
        ],
        scratch_shapes=[
            pltpu.SMEM((1,), jnp.int32),
            pltpu.SMEM((1,), jnp.int32),
            pltpu.SMEM((restore_src.shape[1], n), jnp.int32),
            pltpu.SMEM((restore_src.shape[1], n), jnp.int32),
            pltpu.SMEM((n,), jnp.int32),
            pltpu.SMEM((1,), jnp.int32),
            pltpu.VMEM((taps - 1, channels), bf16),
            pltpu.VMEM((taps - 1, channels), bf16),
            pltpu.VMEM((8, channels), f32),
            pltpu.VMEM((8, channels), bf16),
            pltpu.VMEM((n, new_len, q_width), bf16),
            pltpu.VMEM((blocks, block_len, width), bf16),
            *[pltpu.VMEM((half_n, heads * HD, rows), bf16), pltpu.VMEM((half_n, 8, rows), f32)] * 4,
            pltpu.VMEM(piece, bf16),
            pltpu.VMEM(piece, bf16),
            pltpu.VMEM(piece, bf16),
            both,
        ]
        + [stream] * 5
        + [
            both,
            pltpu.VMEM((new_len, q_width), bf16),
            pltpu.VMEM((2, new_len, width), bf16),
        ]
        + [pltpu.VMEM((2, new_len, channels), bf16)] * 3
        + [
            pltpu.VMEM((1, channels), f32),
            pltpu.VMEM((states, channels), f32),
            pltpu.VMEM((1, channels), f32),
            pltpu.VMEM((taps, channels), f32),
            pltpu.VMEM((1, channels), f32),
            pltpu.VMEM((2 * states, channels), bf16),
            pltpu.VMEM((2, 8 + new_len, width), f32),
            pltpu.VMEM((2, new_len, channels), f32),
            pltpu.VMEM((2 * states, 128), f32),
            pltpu.VMEM((2 * states, 128), f32),
            pltpu.VMEM((2, new_len, 2 * states, HD), f32),
            pltpu.VMEM((2, new_len, width), f32),
            pltpu.VMEM((2, new_len, width), f32),
            pltpu.VMEM((2, new_len, width), f32),
            dma((48,)),
            dma((3, n)),
            dma((3, n)),
            dma((4, half_n)),
            dma((4, half_n)),
            dma((5, half_n)),
            dma((5, half_n)),
            dma((4, chunks)),
            dma((4, chunks)),
            dma((1,)),
            dma((1,)),
        ],
        compiler_params=pltpu.CompilerParams(collective_id=0, has_side_effects=True),
        name="layer",
    )(
        owner_id, readers, jnp.swapaxes(restore_src, 0, 1), jnp.swapaxes(restore_blk, 0, 1), state_src, ctx_blocks,
        queries, new_kv, kv, prefix_ssm, pool_kv, pool_ssm, pool_conv, prefix_conv,
        mamba_x, mamba_z, mamba_dt, dt_bias[None], a_log, bypass_gain[None], conv_w, conv_b[None],
        jnp.swapaxes(w_bc, 0, 1),
    )


def placed_specs():
    return (
        P(("groups", "replica"), None, None, "channel"),
        P(("groups", "replica"), None, None, "channel"),
        P(("groups", "replica"), None, "channel"),
        P(("groups", "replica"), None, "channel"),
        P(("groups", "replica"), None, "channel"),
        P(("groups", "replica"), None, None, "channel"),
        P(("groups", "replica"), None, "channel"),
        P(("groups", "replica"), None, "channel"),
        P("groups"),
        P(("groups", "replica")),
        P("groups", None),
        P("groups", None),
        P("groups"),
        P(("groups", "replica")),
        P(("groups", "replica"), None, None, "channel"),
        P(("groups", "replica"), None, None, "channel"),
        P(("groups", "replica"), None, None, "channel"),
        P("channel"),
        P(None, "channel"),
        P("channel"),
        P(None, "channel"),
        P("channel"),
        P("channel", None),
    )


def solution(mesh):
    return jax.shard_map(
        local,
        mesh=mesh,
        in_specs=placed_specs(),
        out_specs=(
            P(("groups", "replica"), None, None, "channel"),
            P(("groups", "replica"), None, None, "channel"),
        ),
        check_vma=False,
    )
```
